128 devices in a mesh: dp: 16 (over x, z), expert: 8 (over y, core).
Axes of the slice: x: 4, y: 4, z: 4, core: 2. Of those that a mesh axis runs over, the one named last changes fastest.
Arguments:
- tokens: float32 [8192, 1664], P('dp'), may hold values from -6 to 6
- ln_gain: float32 [1664], replicated, may hold values from 0.1 to 1.9
- ln_bias: float32 [1664], replicated, may hold values from -3 to 3
- weight_in: bfloat16 [32, 1664, 8192], P('dp', None, 'expert'), may hold values from -0.15625 to 0.15625
- weight_out: bfloat16 [32, 8192, 1664], P('dp', 'expert'), may hold values from -0.0625 to 0.0625
- expert_ids: int32 [8192, 2], P('dp'), may hold values from 0 to 31, all different within a row; in each aligned block of 512 rows (0 to 511, 512 to 1023, ...) at most 80 rows name the same one
- combine_weights: float32 [8192, 2], P('dp'), may hold values from 0.2 to 1
- owner_ids: int32 [32, 1], replicated, may hold values from 0 to 15; in each aligned block of 32 rows (0 to 31, 32 to 63, ...) at most 4 rows name the same one
Outputs:
- delivered: float32 [16384, 1664], P('dp', 'expert')
The draws below stay inside these ranges and needn't reach their ends.
Inputs may be any that keep to these rules, and one draw needn't show every extreme that they name: `expert_ids`: the two entries of a row differ. In each aligned block of 512 rows no expert is named more than 80 times. `owner_ids`: no owner is named more than 4 times.
All inputs are finite; a program needn't handle non-finite values.
Results may differ from the reference program's by a relative error of at most 0.008.
Values may be sent and summed in bfloat16 or wider, within the bound.
A program may use at most 128 MiB of HBM per device.

```python
import math
import jax
import jax.numpy as jnp
import numpy as np
from jax import lax

D = 1664
FF = 8192
PATCH = 256
TOK_DEV = 512
CAP = 80
OWN_IMG = 4
EXPERTS = 32
TOKENS = 8192
IMAGES = 32
N_DP = 16
N_EXPERT = 8


def block_scale(key, dims, cuts, least, high):
    def one(position, blocks):
        steps = jax.random.uniform(jax.random.fold_in(jax.random.fold_in(key, 6), position), (blocks,), jnp.float32, least / len(cuts), high / len(cuts))
        return jnp.repeat(jnp.exp(steps), dims[position] // blocks).reshape((-1,) + (1,) * (len(dims) - position - 1))

    gain = one(*cuts[0])
    for cut in cuts[1:]:
        gain = gain * one(*cut)
    return gain


def assign_block(own_key, own, number, rows, count, top, reach, slope):
    ranking = jax.random.permutation(own_key, count)
    packed, common = shares(count, rows * top, reach, slope, True), shares(count, rows * top, reach, slope, False)
    places = jnp.arange(count)

    def named(lengths, rotation):
        used = int((lengths > 0).sum())
        fixed = max(1, used // 4)
        passed = fixed + (places - fixed + rotation * (used - fixed)) % max(1, count - fixed)
        return jnp.zeros((count,), jnp.int32).at[ranking[jnp.where(places < fixed, places, passed)]].set(jnp.asarray(lengths, jnp.int32))

    lengths = jnp.where(number % 4 == 0, named(packed, number // 4), named(common, number - number // 4 - 1))
    mixed = jax.random.permutation(jax.random.fold_in(own, 3), count)
    source_of, receiver = mixed[0:count // 2 * 2:2], mixed[1:count // 2 * 2:2]
    room = jnp.minimum(lengths[source_of] - 1, reach - lengths[receiver]) // 2
    room = jnp.where((source_of == ranking[0]) | (receiver == ranking[0]) | (lengths[receiver] == 0), 0, jnp.maximum(room, 0))
    passed = jax.random.randint(jax.random.fold_in(own, 4), (count // 2,), 0, 1 << 20) % (room + 1)
    lengths = lengths.at[source_of].add(-passed).at[receiver].add(passed)
    members = jnp.searchsorted(jnp.cumsum(lengths), jnp.arange(rows * top), side="right").astype(jnp.int32)
    listing = members.reshape(top, rows).T
    listing = listing[jax.random.permutation(jax.random.fold_in(own, 1), rows)]
    rotation = jax.random.randint(jax.random.fold_in(own, 2), (rows, 1), 0, top)
    return jnp.take_along_axis(listing, (jnp.arange(top)[None, :] + rotation) % top, axis=1)


def shares(count, total, reach, slope, full):
    portions = [(1 << 20) // math.isqrt(grade ** slope) + 1 for grade in range(1, count + 1)]
    largest = reach if full else min(reach, max(-(-total // count), total * portions[0] // sum(portions)))
    least = 1 if total - largest >= count - 1 else 0
    counts, surplus = [largest] + [least] * (count - 1), total - largest - least * (count - 1)
    while surplus > 0:
        movable = [i for i in range(1, count) if counts[i] < largest] or [i for i in range(1, count) if counts[i] < reach]
        mass, remaining = sum([portions[i] for i in movable]), surplus
        for i in movable:
            extra = min(reach - counts[i], max(1, remaining * portions[i] // mass), surplus)
            counts[i] = counts[i] + extra
            surplus = surplus - extra
    return np.array(counts)


def noise(key, dims, width, reach, pieces=(), held_as=jnp.bfloat16):
    drawn = width * jax.random.normal(key, dims, jnp.float32)
    if pieces:
        drawn = drawn * block_scale(key, dims, pieces, -0.22, 0.18)
    return jnp.clip(drawn, -reach, reach).astype(held_as)


def setup_inputs(seed: int = 0) -> dict:
    keys = jax.random.split(jax.random.key(seed), 9)
    tokens = noise(keys[0], (TOKENS, D), 1.0, 6.0, ((0, 16),), jnp.float32)
    ln_gain = jnp.clip(1.0 + 0.18 * jax.random.normal(keys[1], (D,), jnp.float32), 0.1, 1.9)
    ln_bias = noise(keys[2], (D,), 0.5, 3.0, (), jnp.float32)
    weight_in = noise(keys[3], (EXPERTS, D, FF), D ** -0.5, 0.15625, ((0, 16), (2, 8)))
    weight_out = noise(keys[4], (EXPERTS, FF, D), FF ** -0.5, 0.0625, ((0, 16), (1, 8)))
    expert_ids_keys = jax.random.split(jax.random.fold_in(keys[5], 1), TOKENS // TOK_DEV)
    expert_ids_turns = jax.random.permutation(jax.random.fold_in(keys[5], 3), TOKENS // TOK_DEV)
    expert_ids = jax.vmap(lambda own, number: assign_block(jax.random.fold_in(keys[5], 2), own, number, TOK_DEV, EXPERTS, 2, CAP, 2))(expert_ids_keys, expert_ids_turns).reshape((TOKENS, 2))
    combine_weights = jnp.clip(0.2 + 0.8 * jax.random.uniform(keys[6], (TOKENS, 2), jnp.float32) ** block_scale(keys[6], (TOKENS, 2), ((0, 16),), -0.2, 0.2), 0.2, 1.0)
    owner_ids_keys = jax.random.split(jax.random.fold_in(keys[7], 1), IMAGES // IMAGES)
    owner_ids_turns = jax.random.permutation(jax.random.fold_in(keys[7], 3), IMAGES // IMAGES)
    owner_ids = jax.vmap(lambda own, number: assign_block(jax.random.fold_in(keys[7], 2), own, number, IMAGES, N_DP, 1, OWN_IMG, 2))(owner_ids_keys, owner_ids_turns).reshape((IMAGES, 1))
    return {"tokens": tokens, "ln_gain": ln_gain, "ln_bias": ln_bias, "weight_in": weight_in, "weight_out": weight_out, "expert_ids": expert_ids, "combine_weights": combine_weights, "owner_ids": owner_ids}


epsilon = 1e-06

def normalize(tokens, ln_gain, ln_bias):
    center = tokens - lax.optimization_barrier(jnp.mean(tokens, axis=1, keepdims=True))
    spread = lax.optimization_barrier(jnp.mean(center * center, axis=1, keepdims=True))
    return center * lax.rsqrt(spread + epsilon) * ln_gain + ln_bias

def reference(tokens, ln_gain, ln_bias, weight_in, weight_out, expert_ids, combine_weights, owner_ids):
    normed = normalize(tokens, ln_gain, ln_bias).astype(jnp.bfloat16)
    flat_ids = expert_ids.reshape(N_DP, TOK_DEV * 2)
    one_hot = (flat_ids[:, :, None] == jnp.arange(EXPERTS, dtype=jnp.int32)[None, None, :]).astype(jnp.int32)
    slots = lax.optimization_barrier(jnp.sum((jnp.cumsum(one_hot, axis=1) - 1) * one_hot, axis=2)).astype(jnp.int32)
    blocks = jnp.arange(N_DP, dtype=jnp.int32)[:, None]
    target = ((flat_ids * N_DP + blocks) * CAP + slots).reshape(TOKENS * 2).astype(jnp.int32)
    rows = jnp.repeat(normed, 2, axis=0)
    buffer = jnp.zeros((EXPERTS * N_DP * CAP, D), jnp.bfloat16).at[target].set(rows)
    buffer = buffer.reshape(EXPERTS, N_DP * CAP, D)
    group = FF // N_EXPERT

    def expert(operands):
        inputs, first, second = operands
        pre = jnp.dot(inputs.astype(jnp.float32), first.astype(jnp.float32), precision=lax.Precision.HIGHEST)
        hidden = jax.nn.gelu(pre, approximate=True).astype(jnp.bfloat16)
        parts = jnp.einsum('rgf,gfd->rgd', hidden.reshape(-1, N_EXPERT, group).astype(jnp.float32), second.reshape(N_EXPERT, group, D).astype(jnp.float32), precision=lax.Precision.HIGHEST)
        rounded = lax.optimization_barrier(parts.astype(jnp.bfloat16))
        return lax.optimization_barrier(jnp.sum(rounded.astype(jnp.float32), axis=1))
    expert_out = lax.map(expert, (buffer, weight_in, weight_out))
    picked = expert_out.reshape(EXPERTS * N_DP * CAP, D)[target].reshape(TOKENS, 2, D)
    finished = tokens + lax.optimization_barrier(jnp.sum(combine_weights[:, :, None] * picked, axis=1))
    owners = owner_ids[:, 0]
    owner_hot = (owners[:, None] == jnp.arange(N_DP, dtype=jnp.int32)[None, :]).astype(jnp.int32)
    offsets = lax.optimization_barrier(jnp.sum((jnp.cumsum(owner_hot, axis=0) - 1) * owner_hot, axis=1)).astype(jnp.int32)
    row_base = (owners * OWN_IMG + offsets) * PATCH
    placed = (row_base[:, None] + jnp.arange(PATCH, dtype=jnp.int32)[None, :]).reshape(IMAGES * PATCH).astype(jnp.int32)
    delivered = jnp.zeros((N_DP * OWN_IMG * PATCH, D), jnp.float32).at[placed].set(finished)
    return delivered
```

```python
import jax
import jax.numpy as jnp
from jax import lax
from jax.experimental import pallas as pl
from jax.experimental.pallas import tpu as pltpu
from jax.sharding import PartitionSpec as P

MESH = pl.DeviceIdType.MESH
F32 = jnp.float32
BF16 = jnp.bfloat16

PATCH = 256
CAP = 80
OWN_IMG = 4
SIDE = 4
epsilon = 1e-06

COMMON = (0, 1)
EVEN = ((2, 2), (1, 3), (3, 1), (2, 1), (3, 2), (0, 3), (1, 0))
ODD = ((1, 1), (3, 3), (0, 2), (2, 3), (1, 2), (2, 0), (3, 0))
OWNED = 7
FIRST = 3
OWN_SLOT = (2, 3, 4, 8, 9, 10, 11)
GUEST_SLOT = (5, 6, 7, 12, 13, 14, 15)
HALF = 8 * CAP


def column_tiles(width, step, body):
    count = width // step

    def one(n, carry):
        body(pl.ds(pl.multiple_of(n * step, 128), step))
        return carry

    lax.fori_loop(0, count, one, 0)
    if count * step < width:
        body(pl.ds(count * step, width - count * step))


def block(index):
    return pl.ds(index * CAP, CAP)


def kernel(
    img,
    tokens,
    gain,
    bias,
    ids_t,
    weights_t,
    base,
    weight_in,
    weight_out,
    delivered,
    normed,
    rank,
    pick,
    gathered,
    x_in,
    w_in,
    w_out,
    hidden,
    out,
    partner,
    ret,
    partial,
    split,
    pair,
    summed,
    others,
    stage_a,
    message,
    stage_b,
    local_sem,
    wx_send,
    wx_recv,
    go_send,
    go_recv,
    fw_send,
    fw_recv,
    pr_send,
    pr_recv,
    rt_send,
    rt_recv,
    rs_send,
    rs_recv,
    da_send,
    da_recv,
    db_send,
    db_recv,
):
    dp = lax.axis_index("dp")
    ex = lax.axis_index("expert")
    x, z = dp // SIDE, dp % SIDE
    y, core = ex // 2, ex % 2
    parity = y % 2
    tok_rows, width = tokens.shape
    local_hidden = weight_in.shape[2]
    share = delivered.shape[1]

    def at_xz(dx, dz):
        return ((x + dx + SIDE) % SIDE) * SIDE + (z + dz + SIDE) % SIDE

    def at_y(dy):
        return ((y + dy + SIDE) % SIDE) * 2 + core

    def owned(j):
        (ax, az), (bx, bz) = EVEN[j], ODD[j]
        return ax + parity * (bx - ax), az + parity * (bz - az)

    def remote(src, dst, send, recv, device):
        return pltpu.make_async_remote_copy(
            src_ref=src,
            dst_ref=dst,
            send_sem=send,
            recv_sem=recv,
            device_id=device,
            device_id_type=MESH,
        )

    barrier = pltpu.get_barrier_semaphore()
    peers = [(at_xz(dx, dz), ex) for dx in range(SIDE) for dz in range(SIDE) if dx or dz]
    peers += [(dp, at_y(dy)) for dy in range(1, SIDE)]
    peers += [(dp, y * 2 + 1 - core)]
    for peer in peers:
        pl.semaphore_signal(barrier, inc=1, device_id=peer, device_id_type=MESH)

    own_in = pltpu.make_async_copy(
        weight_in.at[core], w_in.at[:, pl.ds(0, local_hidden)], local_sem.at[0]
    )
    own_out = pltpu.make_async_copy(
        weight_out.at[core], w_out.at[pl.ds(0, local_hidden), :], local_sem.at[1]
    )
    own_in.start()
    own_out.start()

    def norm_rows(r, carry):
        rows = pl.ds(pl.multiple_of(r * 64, 64), 64)
        value = tokens[rows, :]
        center = value - jnp.mean(value, axis=1, keepdims=True)
        spread = jnp.mean(center * center, axis=1, keepdims=True)
        value = center * lax.rsqrt(spread + epsilon) * gain[...] + bias[...]
        normed[rows, :] = value.astype(BF16)
        return carry

    lax.fori_loop(0, tok_rows // 64, norm_rows, 0)

    experts = rank.shape[0]
    wanted = lax.broadcasted_iota(jnp.int32, (experts, tok_rows), 0)
    named = (ids_t[0:1, :] == wanted) | (ids_t[1:2, :] == wanted)
    earlier = (
        lax.broadcasted_iota(jnp.int32, (tok_rows, tok_rows), 0)
        < lax.broadcasted_iota(jnp.int32, (tok_rows, tok_rows), 1)
    ).astype(F32).astype(BF16)
    before = jnp.dot(named.astype(F32).astype(BF16), earlier, preferred_element_type=F32)
    rank[...] = jnp.where(named, before, 200.0)

    displacements = [(0, 0), COMMON] + [owned(j) for j in range(OWNED)]
    place = lax.broadcasted_iota(jnp.int32, (CAP, tok_rows), 0).astype(F32)

    def expert_of(i):
        return 2 * at_xz(*displacements[i]) + core

    def hit_rows(i):
        return rank[pl.ds(expert_of(i), 1), :] == place

    for i in range(2 + OWNED):
        pick[block(i), :] = hit_rows(i).astype(F32).astype(BF16)

    pl.semaphore_wait(barrier, len(peers))

    other_core = (dp, y * 2 + 1 - core)
    swap_in = remote(
        weight_in.at[1 - core],
        w_in.at[:, pl.ds(local_hidden, local_hidden)],
        wx_send.at[0],
        wx_recv.at[0],
        other_core,
    )
    swap_out = remote(
        weight_out.at[1 - core],
        w_out.at[pl.ds(local_hidden, local_hidden), :],
        wx_send.at[1],
        wx_recv.at[1],
        other_core,
    )
    swap_in.start()
    swap_out.start()

    sends = []
    for i in range(1, 2 + OWNED):
        j = i - 2
        slot = 1 if i == 1 else OWN_SLOT[j]
        sends.append(
            remote(
                gathered.at[block(i - 1), :],
                x_in.at[block(slot), :],
                go_send.at[i - 1],
                go_recv.at[i - 1],
                (at_xz(*displacements[i]), ex),
            )
        )

    def gather(start, stop):
        rows = pl.ds(start * CAP, (stop - start) * CAP)
        to = pl.ds((start - 1) * CAP, (stop - start) * CAP)

        def one(cols):
            gathered[to, cols] = jnp.dot(
                pick[rows, :], normed[:, cols], preferred_element_type=F32
            ).astype(BF16)

        column_tiles(width, 256, one)

    gather(1, 2 + FIRST)
    for i in range(1, 2 + FIRST):
        sends[i - 1].start()
    gather(2 + FIRST, 2 + OWNED)
    for i in range(2 + FIRST, 2 + OWNED):
        sends[i - 1].start()

    def own_block(cols):
        x_in[block(0), cols] = jnp.dot(
            pick[block(0), :], normed[:, cols], preferred_element_type=F32
        ).astype(BF16)

    column_tiles(width, 256, own_block)

    for i in range(2 + OWNED):
        chosen = jnp.where(ids_t[0:1, :] == expert_of(i), weights_t[0:1, :], weights_t[1:2, :])
        pick[block(i), :] = jnp.where(hit_rows(i), chosen, 0.0).astype(BF16)

    forwards = []
    for j in range(OWNED):
        sign = 1 if j % 2 == 0 else -1
        forwards.append(
            remote(
                x_in.at[block(OWN_SLOT[j]), :],
                x_in.at[block(GUEST_SLOT[j]), :],
                fw_send.at[j],
                fw_recv.at[j],
                (dp, at_y(sign)),
            )
        )

    def forward(j):
        sends[j + 1].wait_recv()
        forwards[j].start()

    for j in range(FIRST):
        forward(j)

    def first_matmul(half):
        rows = pl.ds(half * HALF, HALF)

        def one(cols):
            pre = jnp.dot(x_in[rows, :], w_in[:, cols], preferred_element_type=F32)
            hidden[:, cols] = jax.nn.gelu(pre, approximate=True).astype(BF16)

        column_tiles(2 * local_hidden, 256, one)

    def second_matmul(half):
        rows = pl.ds(half * HALF, HALF)

        def one(cols):
            out[rows, cols] = jnp.dot(
                hidden[...], w_out[:, cols], preferred_element_type=F32
            ).astype(BF16)

        column_tiles(width, 256, one)

    to_owner, back = [], []
    for j in range(OWNED):
        sign = 1 if j % 2 == 0 else -1
        to_owner.append(
            remote(
                out.at[block(GUEST_SLOT[j]), :],
                partner.at[block(j), :],
                pr_send.at[j],
                pr_recv.at[j],
                (dp, at_y(-sign)),
            )
        )
        dx, dz = owned(j)
        back.append(
            remote(
                out.at[block(OWN_SLOT[j]), :],
                ret.at[block(2 + j), :],
                rt_send.at[j],
                rt_recv.at[j],
                (at_xz(-dx, -dz), ex),
            )
        )
    back_common = remote(
        out.at[block(1), :],
        ret.at[block(1), :],
        rt_send.at[OWNED],
        rt_recv.at[OWNED],
        (at_xz(-COMMON[0], -COMMON[1]), ex),
    )

    def add_and_send(j):
        to_owner[j].wait_recv()

        def one(cols):
            mine = out[block(OWN_SLOT[j]), cols].astype(F32)
            out[block(OWN_SLOT[j]), cols] = (
                mine + partner[block(j), cols].astype(F32)
            ).astype(BF16)

        column_tiles(width, 832 // 128 * 128, one)
        back[j].start()

    sends[0].wait_recv()
    for j in range(FIRST):
        forwards[j].wait_recv()
    own_in.wait()
    own_out.wait()
    swap_in.wait_recv()
    swap_out.wait_recv()
    first_matmul(0)
    for j in range(FIRST, OWNED):
        forward(j)
    second_matmul(0)
    back_common.start()
    for j in range(FIRST):
        to_owner[j].start()

    for j in range(FIRST, OWNED):
        forwards[j].wait_recv()
    first_matmul(1)
    for j in range(FIRST):
        add_and_send(j)
    ret[block(0), :] = out[block(0), :]
    second_matmul(1)
    for j in range(FIRST, OWNED):
        to_owner[j].start()
    for j in range(FIRST, OWNED):
        add_and_send(j)

    back_common.wait_recv()
    for j in range(OWNED):
        back[j].wait_recv()
    partial[:, pl.ds(width, 128)] = jnp.zeros((tok_rows, 128), F32)

    def combine(cols):
        partial[:, cols] = lax.dot_general(
            pick[...],
            ret[:, cols],
            (((0,), (0,)), ((), ())),
            preferred_element_type=F32,
        )

    column_tiles(width, 256, combine)

    columns = 2 * SIDE

    def cut(r, carry):
        rows = pl.ds(pl.multiple_of(r * 64, 64), 64)
        for c in range(columns):
            split[c % 2, c // 2, rows, :] = partial[rows, c * share : c * share + 256].astype(BF16)
        return carry

    lax.fori_loop(0, tok_rows // 64, cut, 0)
    to_pair = remote(split.at[1 - core], pair, rs_send.at[0], rs_recv.at[0], other_core)
    to_pair.start()
    to_pair.wait_recv()

    def add_pair(r, carry):
        rows = pl.ds(pl.multiple_of(r * 64, 64), 64)
        for c in range(SIDE):
            summed[c, rows, :] = (
                split[core, c, rows, :].astype(F32) + pair[c, rows, :].astype(F32)
            ).astype(BF16)
        return carry

    lax.fori_loop(0, tok_rows // 64, add_pair, 0)
    over_y = []
    for r in range(1, SIDE):
        over_y.append(
            remote(
                summed.at[(y + r) % SIDE],
                others.at[r - 1],
                rs_send.at[r],
                rs_recv.at[r],
                (dp, at_y(r)),
            )
        )
        over_y[-1].start()
    for copy in over_y:
        copy.wait_recv()
    tail = share - 128
    for i in range(tok_rows // PATCH):
        for r in range(PATCH // 64):
            rows = pl.ds(i * PATCH + r * 64, 64)
            total = summed[y, rows, :].astype(F32)
            for k in range(SIDE - 1):
                total = total + others[k, rows, :].astype(F32)
            to = pl.ds(r * 64, 64)
            stage_a[0, i, to, :] = (total[:, :128] + base[rows, 0:128]).astype(BF16)
            stage_a[1, i, to, 0:tail] = (
                total[:, 128:share] + base[rows, 128:share]
            ).astype(BF16)

    imgs = tok_rows // PATCH

    def along(h, first, step):
        if (h == 0) == first:
            return (at_xz(step, 0), ex)
        return (at_xz(0, step), ex)

    gathers = []
    for h in range(2):
        for r in range(1, SIDE):
            k = h * 3 + r - 1
            gathers.append(
                remote(
                    stage_a.at[h, pl.ds(0, imgs)],
                    stage_a.at[h, pl.ds(imgs * r, imgs)],
                    da_send.at[k],
                    da_recv.at[k],
                    along(h, True, r),
                )
            )
            gathers[-1].start()
    for copy in gathers:
        copy.wait_recv()

    def source_of(owner, j):
        index = img[owner * OWN_IMG + j]
        held = jnp.maximum(index, 0)
        device = held // imgs
        return index, device // SIDE, device % SIDE, held % imgs

    delivers = []
    for q in (1, 3, 2, 0):
        for h in range(2):
            owner = along(h, False, q)[0]
            for j in range(OWN_IMG):
                _, from_x, from_z, which = source_of(owner, j)
                r = (x - from_x + SIDE) % SIDE if h == 0 else (z - from_z + SIDE) % SIDE
                value = stage_a[h, r * imgs + which]
                if q == 0:
                    stage_b[h, j] = value
                else:
                    message[h, q - 1, j] = value
            if q:
                k = h * 3 + q - 1
                delivers.append(
                    remote(
                        message.at[h, q - 1],
                        stage_b.at[h, pl.ds(OWN_IMG * q, OWN_IMG)],
                        db_send.at[k],
                        db_recv.at[k],
                        along(h, False, q),
                    )
                )
                delivers[-1].start()
    for copy in delivers:
        copy.wait_recv()
    for j in range(OWN_IMG):
        index, from_x, from_z, _ = source_of(dp, j)
        there = index >= 0
        rows = pl.ds(j * PATCH, PATCH)
        first = stage_b[0, (z - from_z + SIDE) % SIDE * OWN_IMG + j].astype(F32)
        delivered[rows, 0:128] = jnp.where(there, first, 0.0)
        second = stage_b[1, (x - from_x + SIDE) % SIDE * OWN_IMG + j].astype(F32)
        delivered[rows, 128:share] = jnp.where(there, second, 0.0)[:, :tail]

    for copy in (
        [swap_in, swap_out]
        + sends
        + forwards
        + to_owner
        + back
        + [back_common, to_pair]
        + over_y
        + gathers
        + delivers
    ):
        copy.wait_send()


def shards(tokens, ln_gain, ln_bias, weight_in, weight_out, expert_ids, combine_weights, owner_ids):
    groups = lax.axis_size("dp")
    columns = lax.axis_size("expert")
    tok_rows, width = tokens.shape
    share = width // columns
    hidden = 2 * weight_in.shape[2]
    experts = weight_in.shape[0] * groups

    owners = owner_ids[:, 0]
    images = owners.shape[0]
    order = jnp.arange(images, dtype=jnp.int32)
    same = (owners[:, None] == owners[None, :]) & (order[None, :] < order[:, None])
    place = owners * OWN_IMG + jnp.sum(same.astype(jnp.int32), axis=1)
    slots = jnp.arange(groups * OWN_IMG, dtype=jnp.int32)
    img = jnp.max(
        jnp.where(place[None, :] == slots[:, None], order[None, :], -1), axis=1
    ).astype(jnp.int32)
    base = lax.dynamic_slice_in_dim(tokens, lax.axis_index("expert") * share, share, axis=1)

    def vmem(shape, dtype=BF16):
        return pltpu.VMEM(shape, dtype)

    def sems(count):
        return pltpu.SemaphoreType.DMA((count,))

    whole = pl.BlockSpec(memory_space=pltpu.VMEM)
    scratch = [
        vmem((tok_rows, width)),
        vmem((experts, tok_rows), F32),
        vmem((9 * CAP, tok_rows)),
        vmem((8 * CAP, width)),
        vmem((16 * CAP, width)),
        vmem((width, hidden)),
        vmem((hidden, width)),
        vmem((HALF, hidden)),
        vmem((16 * CAP, width)),
        vmem((OWNED * CAP, width)),
        vmem((9 * CAP, width)),
        vmem((tok_rows, width + 128), F32),
        vmem((2, SIDE, tok_rows, 256)),
        vmem((SIDE, tok_rows, 256)),
        vmem((SIDE, tok_rows, 256)),
        vmem((SIDE - 1, tok_rows, 256)),
        vmem((2, 8, PATCH, 128)),
        vmem((2, SIDE - 1, OWN_IMG, PATCH, 128)),
        vmem((2, SIDE * OWN_IMG, PATCH, 128)),
    ]
    for count in (2, 2, 2, 8, 8, 7, 7, 7, 7, 8, 8, 4, 4, 6, 6, 6, 6):
        scratch.append(sems(count))
    return pl.pallas_call(
        kernel,
        out_shape=jax.ShapeDtypeStruct((OWN_IMG * PATCH, share), F32),
        in_specs=[pl.BlockSpec(memory_space=pltpu.SMEM)]
        + [whole] * 6
        + [pl.BlockSpec(memory_space=pl.ANY)] * 2,
        out_specs=whole,
        scratch_shapes=scratch,
        compiler_params=pltpu.CompilerParams(
            collective_id=0, has_side_effects=True, vmem_limit_bytes=67043328
        ),
    )(
        img,
        tokens,
        ln_gain.reshape(1, width),
        ln_bias.reshape(1, width),
        expert_ids.T,
        combine_weights.T,
        base,
        weight_in,
        weight_out,
    )


def solution(mesh):
    return jax.shard_map(
        shards,
        mesh=mesh,
        in_specs=(
            P("dp", None),
            P(),
            P(),
            P("dp", None, "expert"),
            P("dp", "expert", None),
            P("dp", None),
            P("dp", None),
            P(),
        ),
        out_specs=P("dp", "expert"),
        check_vma=False,
    )
```

```python
import jax
import jax.numpy as jnp
from jax import lax
from jax.experimental import pallas as pl
from jax.experimental.pallas import tpu as pltpu
from jax.sharding import PartitionSpec as P

MESH = pl.DeviceIdType.MESH
F32 = jnp.float32
BF16 = jnp.bfloat16

PATCH = 256
CAP = 80
OWN_IMG = 4
SIDE = 4
epsilon = 1e-06

COMMON = (0, 1)
EVEN = ((2, 2), (1, 3), (3, 1), (2, 1), (3, 2), (0, 3), (1, 0))
ODD = ((1, 1), (3, 3), (0, 2), (2, 3), (1, 2), (2, 0), (3, 0))
OWNED = 7
OWN_SLOT = (2, 4, 5, 8, 9, 12, 13)
GUEST_SLOT = (3, 6, 7, 10, 11, 14, 15)
IN_CHUNK = ((0,), (1, 2), (3, 4), (5, 6))
CHUNK = 4 * CAP
EARLY = 7 * CAP


def column_tiles(width, step, body):
    count = width // step

    def one(n, carry):
        body(pl.ds(pl.multiple_of(n * step, 128), step))
        return carry

    lax.fori_loop(0, count, one, 0)
    if count * step < width:
        body(pl.ds(count * step, width - count * step))


def block(index):
    return pl.ds(index * CAP, CAP)


def kernel(
    owners,
    tokens,
    gain,
    bias,
    ids_t,
    weights_t,
    weight_in,
    weight_out,
    delivered,
    img,
    base,
    normed,
    rank,
    pick,
    gathered,
    x_in,
    w_in,
    w_out,
    hidden,
    out,
    partner,
    ret,
    partial,
    split,
    pair,
    summed,
    others,
    stage_a0,
    stage_a1,
    message,
    stage_b0,
    stage_b1,
    local_sem,
    wx_send,
    wx_recv,
    go_send,
    go_recv,
    fw_send,
    fw_recv,
    pr_send,
    pr_recv,
    rt_send,
    rt_recv,
    rs_send,
    rs_recv,
    da_send,
    da_recv,
    db_send,
    db_recv,
):
    stage_a, stage_b = (stage_a0, stage_a1), (stage_b0, stage_b1)
    dp = lax.axis_index("dp")
    ex = lax.axis_index("expert")
    x, z = dp // SIDE, dp % SIDE
    y, core = ex // 2, ex % 2
    parity = y % 2
    tok_rows, width = tokens.shape
    local_hidden = weight_in.shape[2]
    share = delivered.shape[1]

    def at_xz(dx, dz):
        return ((x + dx + SIDE) % SIDE) * SIDE + (z + dz + SIDE) % SIDE

    def at_y(dy):
        return ((y + dy + SIDE) % SIDE) * 2 + core

    def owned(j):
        (ax, az), (bx, bz) = EVEN[j], ODD[j]
        return ax + parity * (bx - ax), az + parity * (bz - az)

    def remote(src, dst, send, recv, device):
        return pltpu.make_async_remote_copy(
            src_ref=src,
            dst_ref=dst,
            send_sem=send,
            recv_sem=recv,
            device_id=device,
            device_id_type=MESH,
        )

    started, heard = [], []

    def go(copy):
        copy.start()
        started.append(copy)

    def hear(copy):
        copy.wait_recv()
        heard.append(copy)

    def finish():
        for copy in started:
            copy.wait_send()


    barrier = pltpu.get_barrier_semaphore()
    peers = [(at_xz(dx, dz), ex) for dx in range(SIDE) for dz in range(SIDE) if dx or dz]
    peers += [(dp, at_y(dy)) for dy in range(1, SIDE)]
    peers += [(dp, y * 2 + 1 - core)]
    for peer in peers:
        pl.semaphore_signal(barrier, inc=1, device_id=peer, device_id_type=MESH)

    own_in = pltpu.make_async_copy(
        weight_in.at[core], w_in.at[:, pl.ds(0, local_hidden)], local_sem.at[0]
    )
    own_out = pltpu.make_async_copy(
        weight_out.at[core], w_out.at[pl.ds(0, local_hidden), :], local_sem.at[1]
    )
    own_in.start()
    own_out.start()

    lanes = [pl.ds(c * 128, 128) for c in range(width // 128)]

    def norm_rows(r, carry):
        rows = pl.ds(pl.multiple_of(r * 64, 64), 64)
        total = tokens[rows, lanes[0]]
        for cols in lanes[1:]:
            total = total + tokens[rows, cols]
        mean = jnp.sum(total, axis=1, keepdims=True) / width
        total = jnp.zeros((64, 128), F32)
        for cols in lanes:
            center = tokens[rows, cols] - mean
            total = total + center * center
        scale = lax.rsqrt(jnp.sum(total, axis=1, keepdims=True) / width + epsilon)
        for c, cols in enumerate(lanes):
            value = (tokens[rows, cols] - mean) * scale * gain[c : c + 1, :] + bias[c : c + 1, :]
            normed[rows, cols] = value.astype(BF16)
        return carry

    lax.fori_loop(0, tok_rows // 64, norm_rows, 0, unroll=2)

    experts = rank.shape[0]
    wanted = lax.broadcasted_iota(jnp.int32, (experts, tok_rows), 0)
    named = (ids_t[0:1, :] == wanted) | (ids_t[1:2, :] == wanted)
    earlier = (
        lax.broadcasted_iota(jnp.int32, (tok_rows, tok_rows), 0)
        < lax.broadcasted_iota(jnp.int32, (tok_rows, tok_rows), 1)
    ).astype(F32).astype(BF16)
    before = jnp.dot(named.astype(F32).astype(BF16), earlier, preferred_element_type=F32)
    rank[...] = jnp.where(named, before, 200.0)

    displacements = [(0, 0), COMMON] + [owned(j) for j in range(OWNED)]
    place = lax.broadcasted_iota(jnp.int32, (CAP, tok_rows), 0).astype(F32)

    def expert_of(i):
        return 2 * at_xz(*displacements[i]) + core

    def hit_rows(i):
        return rank[pl.ds(expert_of(i), 1), :] == place

    for i in range(2 + OWNED):
        pick[block(i), :] = hit_rows(i).astype(F32).astype(BF16)

    pl.semaphore_wait(barrier, len(peers))

    other_core = (dp, y * 2 + 1 - core)
    swap_in = remote(
        weight_in.at[1 - core],
        w_in.at[:, pl.ds(local_hidden, local_hidden)],
        wx_send.at[0],
        wx_recv.at[0],
        other_core,
    )
    swap_out = remote(
        weight_out.at[1 - core],
        w_out.at[pl.ds(local_hidden, local_hidden), :],
        wx_send.at[1],
        wx_recv.at[1],
        other_core,
    )
    go(swap_in)
    go(swap_out)

    sends = []
    for i in range(1, 2 + OWNED):
        j = i - 2
        slot = 1 if i == 1 else OWN_SLOT[j]
        sends.append(
            remote(
                gathered.at[block(i - 1), :],
                x_in.at[block(slot), :],
                go_send.at[i - 1],
                go_recv.at[i - 1],
                (at_xz(*displacements[i]), ex),
            )
        )

    def gather(start, stop):
        rows = pl.ds(start * CAP, (stop - start) * CAP)
        to = pl.ds((start - 1) * CAP, (stop - start) * CAP)

        def one(cols):
            gathered[to, cols] = jnp.dot(
                pick[rows, :], normed[:, cols], preferred_element_type=F32
            ).astype(BF16)

        column_tiles(width, 256, one)

    for start, end in ((1, 3), (3, 5), (5, 9)):
        gather(start, end)
        for i in range(start, end):
            go(sends[i - 1])

    def own_block(cols):
        x_in[block(0), cols] = jnp.dot(
            pick[block(0), :], normed[:, cols], preferred_element_type=F32
        ).astype(BF16)

    column_tiles(width, 256, own_block)

    for i in range(2 + OWNED):
        chosen = jnp.where(ids_t[0:1, :] == expert_of(i), weights_t[0:1, :], weights_t[1:2, :])
        pick[block(i), :] = jnp.where(hit_rows(i), chosen, 0.0).astype(BF16)

    forwards = []
    for j in range(OWNED):
        sign = 1 if j % 2 == 0 else -1
        forwards.append(
            remote(
                x_in.at[block(OWN_SLOT[j]), :],
                x_in.at[block(GUEST_SLOT[j]), :],
                fw_send.at[j],
                fw_recv.at[j],
                (dp, at_y(sign)),
            )
        )

    def forward(j):
        hear(sends[j + 1])
        go(forwards[j])

    for j in range(3):
        forward(j)

    for c in range(2 * SIDE):

        @pl.when(ex == c)
        def _():
            def one(r, carry):
                rows = pl.ds(pl.multiple_of(r * 64, 64), 64)
                base[rows, :] = tokens[rows, c * share : (c + 1) * share]
                return carry

            lax.fori_loop(0, tok_rows // 64, one, 0)

    near = [dp] + [at_xz(0, q) for q in range(1, SIDE)] + [at_xz(q, 0) for q in range(1, SIDE)]

    def note(i, carry):
        owner, new = owners[i], []
        for w, candidate in enumerate(near):
            count, held = carry[w][0], carry[w][1:]
            hit = owner == candidate
            held = [jnp.where(hit & (count == k), i, held[k]) for k in range(OWN_IMG)]
            new.append((count + hit.astype(jnp.int32), *held))
        return tuple(new)

    none = jnp.int32(-1)
    noted = lax.fori_loop(
        0, owners.shape[0], note, ((jnp.int32(0),) + (none,) * OWN_IMG,) * len(near)
    )
    for w in range(len(near)):
        for k in range(OWN_IMG):
            img[w * OWN_IMG + k] = noted[w][1 + k]

    def first_matmul(c):
        pre = jnp.dot(x_in[pl.ds(c * CHUNK, CHUNK), :], w_in[...], preferred_element_type=F32)
        hidden[...] = jax.nn.gelu(pre, approximate=True).astype(BF16)

    def second_matmul(c):
        out[pl.ds(c * CHUNK, CHUNK), :] = jnp.dot(
            hidden[...], w_out[...], preferred_element_type=F32
        ).astype(BF16)

    to_owner, back = [], []
    for j in range(OWNED):
        sign = 1 if j % 2 == 0 else -1
        to_owner.append(
            remote(
                out.at[block(GUEST_SLOT[j]), :],
                partner.at[block(j), :],
                pr_send.at[j],
                pr_recv.at[j],
                (dp, at_y(-sign)),
            )
        )
        dx, dz = owned(j)
        back.append(
            remote(
                out.at[block(OWN_SLOT[j]), :],
                ret.at[block(2 + j), :],
                rt_send.at[j],
                rt_recv.at[j],
                (at_xz(-dx, -dz), ex),
            )
        )
    back_common = remote(
        out.at[block(1), :],
        ret.at[block(1), :],
        rt_send.at[OWNED],
        rt_recv.at[OWNED],
        (at_xz(-COMMON[0], -COMMON[1]), ex),
    )

    def add_and_send(j):
        hear(to_owner[j])

        def one(cols):
            mine = out[block(OWN_SLOT[j]), cols].astype(F32)
            out[block(OWN_SLOT[j]), cols] = (
                mine + partner[block(j), cols].astype(F32)
            ).astype(BF16)

        column_tiles(width, 768, one)
        go(back[j])

    hear(sends[0])
    for c, members in enumerate(IN_CHUNK):
        for j in members:
            hear(forwards[j])
        if c == 0:
            own_in.wait()
            hear(swap_in)
        first_matmul(c)
        if c < 2:
            forward(2 * c + 3)
        if c == 0:
            own_out.wait()
            hear(swap_out)
        else:
            for j in IN_CHUNK[c - 1]:
                add_and_send(j)
        second_matmul(c)
        for j in members:
            go(to_owner[j])
        if c < 2:
            forward(2 * c + 4)
        if c == 0:
            go(back_common)
            ret[block(0), :] = out[block(0), :]
    for j in IN_CHUNK[-1]:
        add_and_send(j)

    hear(back_common)
    for j in range(5):
        hear(back[j])
    partial[:, pl.ds(width, 128)] = jnp.zeros((tok_rows, 128), F32)

    def combine(first):
        rows = pl.ds(0, EARLY) if first else pl.ds(EARLY, pick.shape[0] - EARLY)

        def one(cols):
            value = lax.dot_general(
                pick[rows, :],
                ret[rows, cols],
                (((0,), (0,)), ((), ())),
                preferred_element_type=F32,
            )
            partial[:, cols] = value if first else partial[:, cols] + value

        column_tiles(width, 256, one)

    combine(True)
    for j in range(5, OWNED):
        hear(back[j])
    combine(False)

    columns = 2 * SIDE
    imgs = tok_rows // PATCH
    part = PATCH // 2

    def row_blocks(p, body):
        for i in range(imgs):

            def one(r, carry):
                off = pl.multiple_of(r * 64, 64)
                body(
                    i,
                    off,
                    pl.ds(pl.multiple_of(i * PATCH + p * part + r * 64, 64), 64),
                    pl.ds(pl.multiple_of(i * part + r * 64, 64), 64),
                )
                return carry

            lax.fori_loop(0, part // 64, one, 0)

    to_pair = []
    for p in range(2):

        def cut(i, off, rows, to):
            for c in range(columns):
                split[c % 2, c // 2, p, to, :] = partial[
                    rows, c * share : c * share + 256
                ].astype(BF16)

        row_blocks(p, cut)
        to_pair.append(
            remote(
                split.at[1 - core, :, p],
                pair.at[:, p],
                rs_send.at[p],
                rs_recv.at[p],
                other_core,
            )
        )
        go(to_pair[-1])
    over_y = []
    for p in range(2):
        hear(to_pair[p])

        def add_pair(i, off, rows, to):
            for c in range(SIDE):
                summed[c, p, to, :] = (
                    split[core, c, p, to, :].astype(F32) + pair[c, p, to, :].astype(F32)
                ).astype(BF16)

        row_blocks(p, add_pair)
        for r in (1, 3, 2):
            over_y.append(
                remote(
                    summed.at[(y + r) % SIDE, p],
                    others.at[r - 1, p],
                    rs_send.at[2 + p * 3 + r - 1],
                    rs_recv.at[2 + p * 3 + r - 1],
                    (dp, at_y(r)),
                )
            )
            go(over_y[-1])
    tail = share - 128

    def along(h, first, step):
        if (h == 0) == first:
            return (at_xz(step, 0), ex)
        return (at_xz(0, step), ex)

    gathers = []
    for p in range(2):
        for copy in over_y[3 * p : 3 * p + 3]:
            hear(copy)

        def total_up(i, off, rows, to):
            total = summed[y, p, to, :].astype(F32)
            for k in range(SIDE - 1):
                total = total + others[k, p, to, :].astype(F32)
            at = pl.ds(off, 64)
            stage_a[p][0, i, at, :] = (total[:, :128] + base[rows, 0:128]).astype(BF16)
            stage_a[p][1, i, at, 0:tail] = (
                total[:, 128:share] + base[rows, 128:share]
            ).astype(BF16)

        row_blocks(p, total_up)
        for r in (1, 3, 2):
            for h in range(2):
                k = (p * 2 + h) * 3 + r - 1
                gathers.append(
                    remote(
                        stage_a[p].at[h, pl.ds(0, imgs)],
                        stage_a[p].at[h, pl.ds(imgs * r, imgs)],
                        da_send.at[k],
                        da_recv.at[k],
                        along(h, True, r),
                    )
                )
                go(gathers[-1])

    def source_of(w, j):
        index = img[w * OWN_IMG + j]
        held = jnp.maximum(index, 0)
        device = held // imgs
        return index, device // SIDE, device % SIDE, held % imgs

    delivers = []
    for p in range(2):
        for copy in gathers[6 * p : 6 * p + 6]:
            hear(copy)
        for q in (1, 3, 2, 0):
            for h in range(2):
                w = q if h == 0 or q == 0 else SIDE - 1 + q
                for j in range(OWN_IMG):
                    _, from_x, from_z, which = source_of(w, j)
                    r = (x - from_x + SIDE) % SIDE if h == 0 else (z - from_z + SIDE) % SIDE
                    value = stage_a[p][h, r * imgs + which]
                    if q == 0:
                        stage_b[p][h, j] = value
                    else:
                        message[h, p, q - 1, j] = value
                if q:
                    k = (p * 2 + h) * 3 + q - 1
                    delivers.append(
                        remote(
                            message.at[h, p, q - 1],
                            stage_b[p].at[h, pl.ds(OWN_IMG * q, OWN_IMG)],
                            db_send.at[k],
                            db_recv.at[k],
                            along(h, False, q),
                        )
                    )
                    go(delivers[-1])
    for p in range(2):
        for copy in delivers[6 * p : 6 * p + 6]:
            hear(copy)
        for j in range(OWN_IMG):
            index, from_x, from_z, _ = source_of(0, j)
            there = index >= 0
            rows = pl.ds(j * PATCH + p * part, part)
            first = stage_b[p][0, (z - from_z + SIDE) % SIDE * OWN_IMG + j].astype(F32)
            delivered[rows, 0:128] = jnp.where(there, first, 0.0).astype(BF16)
            second = stage_b[p][1, (x - from_x + SIDE) % SIDE * OWN_IMG + j].astype(F32)
            delivered[rows, 128:share] = jnp.where(there, second, 0.0)[:, :tail].astype(BF16)
    finish()


def shards(tokens, ln_gain, ln_bias, weight_in, weight_out, expert_ids, combine_weights, owner_ids):
    groups = lax.axis_size("dp")
    columns = lax.axis_size("expert")
    tok_rows, width = tokens.shape
    share = width // columns
    hidden = 2 * weight_in.shape[2]
    experts = weight_in.shape[0] * groups

    def vmem(shape, dtype=BF16):
        return pltpu.VMEM(shape, dtype)

    def sems(count):
        return pltpu.SemaphoreType.DMA((count,))

    whole = pl.BlockSpec(memory_space=pltpu.VMEM)
    scratch = [
        pltpu.SMEM((7 * OWN_IMG,), jnp.int32),
        vmem((tok_rows, share), F32),
        vmem((tok_rows, width)),
        vmem((experts, tok_rows), F32),
        vmem((9 * CAP, tok_rows)),
        vmem((8 * CAP, width)),
        vmem((16 * CAP, width)),
        vmem((width, hidden)),
        vmem((hidden, width)),
        vmem((CHUNK, hidden)),
        vmem((16 * CAP, width)),
        vmem((OWNED * CAP, width)),
        vmem((9 * CAP, width)),
        vmem((tok_rows, width + 128), F32),
        vmem((2, SIDE, 2, tok_rows // 2, 256)),
        vmem((SIDE, 2, tok_rows // 2, 256)),
        vmem((SIDE, 2, tok_rows // 2, 256)),
        vmem((SIDE - 1, 2, tok_rows // 2, 256)),
        vmem((2, 8, PATCH // 2, 128)),
        vmem((2, 8, PATCH // 2, 128)),
        vmem((2, 2, SIDE - 1, OWN_IMG, PATCH // 2, 128)),
        vmem((2, SIDE * OWN_IMG, PATCH // 2, 128)),
        vmem((2, SIDE * OWN_IMG, PATCH // 2, 128)),
    ]
    for count in (2, 2, 2, 8, 8, 7, 7, 7, 7, 8, 8, 8, 8, 12, 12, 12, 12):
        scratch.append(sems(count))
    return pl.pallas_call(
        kernel,
        out_shape=jax.ShapeDtypeStruct((OWN_IMG * PATCH, share), BF16),
        in_specs=[pl.BlockSpec(memory_space=pltpu.SMEM)]
        + [whole] * 5
        + [pl.BlockSpec(memory_space=pl.ANY)] * 2,
        out_specs=whole,
        scratch_shapes=scratch,
        compiler_params=pltpu.CompilerParams(
            collective_id=0, has_side_effects=True, vmem_limit_bytes=67043328
        ),
    )(
        owner_ids.reshape(-1),
        tokens,
        ln_gain.reshape(-1, 128),
        ln_bias.reshape(-1, 128),
        expert_ids.T,
        combine_weights.T,
        weight_in,
        weight_out,
    ).astype(F32)


def solution(mesh):
    return jax.shard_map(
        shards,
        mesh=mesh,
        in_specs=(
            P("dp", None),
            P(),
            P(),
            P("dp", None, "expert"),
            P("dp", "expert", None),
            P("dp", None),
            P("dp", None),
            P(),
        ),
        out_specs=P("dp", "expert"),
        check_vma=False,
    )
```

```python
import jax
import jax.numpy as jnp
from jax import lax
from jax.experimental import pallas as pl
from jax.experimental.pallas import tpu as pltpu
from jax.sharding import PartitionSpec as P

MESH = pl.DeviceIdType.MESH
F32 = jnp.float32
BF16 = jnp.bfloat16

PATCH = 256
CAP = 80
OWN_IMG = 4
SIDE = 4
epsilon = 1e-06

NEAR = ((0, 1), (0, 3), (1, 0), (3, 0), (1, 3))
EVEN = ((2, 2), (3, 1), (3, 3), (1, 2), (2, 1))
ODD = ((1, 1), (0, 2), (2, 0), (2, 3), (3, 2))
NEARS, OWNED = 5, 5
NEAR_SLOT = (1, 2, 3, 4, 5)
OWN_SLOT = (6, 8, 9, 12, 13)
GUEST_SLOT = (7, 10, 11, 14, 15)
SENT = NEARS + OWNED
CHUNK = 4 * CAP
EARLY = 9 * CAP


def column_tiles(width, step, body):
    count = width // step

    def one(n, carry):
        body(pl.ds(pl.multiple_of(n * step, 128), step))
        return carry

    lax.fori_loop(0, count, one, 0)
    if count * step < width:
        body(pl.ds(count * step, width - count * step))


def block(index):
    return pl.ds(index * CAP, CAP)


def kernel(
    owners,
    tokens,
    gain,
    bias,
    ids_t,
    weights_t,
    weight_in,
    weight_out,
    delivered,
    img,
    base,
    normed,
    rank,
    pick,
    gathered,
    x_in,
    w_in,
    w_out,
    hidden,
    out,
    partner,
    ret,
    partial,
    split,
    pair,
    summed,
    others,
    stage_a0,
    stage_a1,
    message,
    stage_b0,
    stage_b1,
    local_sem,
    wx_send,
    wx_recv,
    go_send,
    go_recv,
    fw_send,
    fw_recv,
    pr_send,
    pr_recv,
    rt_send,
    rt_recv,
    rs_send,
    rs_recv,
    da_send,
    da_recv,
    db_send,
    db_recv,
):
    stage_a, stage_b = (stage_a0, stage_a1), (stage_b0, stage_b1)
    dp = lax.axis_index("dp")
    ex = lax.axis_index("expert")
    x, z = dp // SIDE, dp % SIDE
    y, core = ex // 2, ex % 2
    parity = y % 2
    tok_rows, width = tokens.shape
    local_hidden = weight_in.shape[2]
    share = delivered.shape[1]

    def at_xz(dx, dz):
        return ((x + dx + SIDE) % SIDE) * SIDE + (z + dz + SIDE) % SIDE

    def at_y(dy):
        return ((y + dy + SIDE) % SIDE) * 2 + core

    def owned(j):
        (ax, az), (bx, bz) = EVEN[j], ODD[j]
        return ax + parity * (bx - ax), az + parity * (bz - az)

    def remote(src, dst, send, recv, device):
        return pltpu.make_async_remote_copy(
            src_ref=src,
            dst_ref=dst,
            send_sem=send,
            recv_sem=recv,
            device_id=device,
            device_id_type=MESH,
        )

    started, heard = [], []

    def go(copy):
        copy.start()
        started.append(copy)

    def hear(copy):
        copy.wait_recv()
        heard.append(copy)

    def finish():
        for copy in started:
            copy.wait_send()


    barrier = pltpu.get_barrier_semaphore()
    peers = [(at_xz(dx, dz), ex) for dx in range(SIDE) for dz in range(SIDE) if dx or dz]
    peers += [(dp, at_y(dy)) for dy in range(1, SIDE)]
    peers += [(dp, y * 2 + 1 - core)]
    for peer in peers:
        pl.semaphore_signal(barrier, inc=1, device_id=peer, device_id_type=MESH)

    own_in = pltpu.make_async_copy(
        weight_in.at[core], w_in.at[:, pl.ds(0, local_hidden)], local_sem.at[0]
    )
    own_out = pltpu.make_async_copy(
        weight_out.at[core], w_out.at[pl.ds(0, local_hidden), :], local_sem.at[1]
    )
    own_in.start()
    own_out.start()

    lanes = [pl.ds(c * 128, 128) for c in range(width // 128)]

    def norm_rows(r, carry):
        rows = pl.ds(pl.multiple_of(r * 64, 64), 64)
        total = tokens[rows, lanes[0]]
        for cols in lanes[1:]:
            total = total + tokens[rows, cols]
        mean = jnp.sum(total, axis=1, keepdims=True) / width
        total = jnp.zeros((64, 128), F32)
        for cols in lanes:
            center = tokens[rows, cols] - mean
            total = total + center * center
        scale = lax.rsqrt(jnp.sum(total, axis=1, keepdims=True) / width + epsilon)
        for c, cols in enumerate(lanes):
            value = (tokens[rows, cols] - mean) * scale * gain[c : c + 1, :] + bias[c : c + 1, :]
            normed[rows, cols] = value.astype(BF16)
        return carry

    lax.fori_loop(0, tok_rows // 64, norm_rows, 0, unroll=2)

    experts = rank.shape[0]
    wanted = lax.broadcasted_iota(jnp.int32, (experts, tok_rows), 0)
    named = (ids_t[0:1, :] == wanted) | (ids_t[1:2, :] == wanted)
    earlier = (
        lax.broadcasted_iota(jnp.int32, (tok_rows, tok_rows), 0)
        < lax.broadcasted_iota(jnp.int32, (tok_rows, tok_rows), 1)
    ).astype(F32).astype(BF16)
    before = jnp.dot(named.astype(F32).astype(BF16), earlier, preferred_element_type=F32)
    rank[...] = jnp.where(named, before, 200.0)

    displacements = [(0, 0), *NEAR] + [owned(j) for j in range(OWNED)]
    place = lax.broadcasted_iota(jnp.int32, (CAP, tok_rows), 0).astype(F32)

    def expert_of(i):
        return 2 * at_xz(*displacements[i]) + core

    def hit_rows(i):
        return rank[pl.ds(expert_of(i), 1), :] == place

    for i in range(1 + SENT):
        pick[block(i), :] = hit_rows(i).astype(F32).astype(BF16)

    pl.semaphore_wait(barrier, len(peers))

    other_core = (dp, y * 2 + 1 - core)
    swap_in = remote(
        weight_in.at[1 - core],
        w_in.at[:, pl.ds(local_hidden, local_hidden)],
        wx_send.at[0],
        wx_recv.at[0],
        other_core,
    )
    swap_out = remote(
        weight_out.at[1 - core],
        w_out.at[pl.ds(local_hidden, local_hidden), :],
        wx_send.at[1],
        wx_recv.at[1],
        other_core,
    )
    go(swap_in)
    go(swap_out)

    sends = []
    for i in range(SENT):
        slot = (NEAR_SLOT + OWN_SLOT)[i]
        sends.append(
            remote(
                gathered.at[block(i), :],
                x_in.at[block(slot), :],
                go_send.at[i],
                go_recv.at[i],
                (at_xz(*displacements[i + 1]), ex),
            )
        )

    def gather(start, stop):
        rows = pl.ds(start * CAP, (stop - start) * CAP)
        to = pl.ds((start - 1) * CAP, (stop - start) * CAP)

        def one(cols):
            gathered[to, cols] = jnp.dot(
                pick[rows, :], normed[:, cols], preferred_element_type=F32
            ).astype(BF16)

        column_tiles(width, 256, one)

    gather(1, 4)
    for i in range(3):
        go(sends[i])
    gather(4, 1 + SENT)
    for i in (5, 3, 4, 6, 7, 8, 9):
        go(sends[i])

    def own_block(cols):
        x_in[block(0), cols] = jnp.dot(
            pick[block(0), :], normed[:, cols], preferred_element_type=F32
        ).astype(BF16)

    column_tiles(width, 256, own_block)

    for i in range(1 + SENT):
        chosen = jnp.where(ids_t[0:1, :] == expert_of(i), weights_t[0:1, :], weights_t[1:2, :])
        pick[block(i), :] = jnp.where(hit_rows(i), chosen, 0.0).astype(BF16)

    forwards = []
    for j in range(OWNED):
        sign = 1 if j % 2 == 0 else -1
        forwards.append(
            remote(
                x_in.at[block(OWN_SLOT[j]), :],
                x_in.at[block(GUEST_SLOT[j]), :],
                fw_send.at[j],
                fw_recv.at[j],
                (dp, at_y(sign)),
            )
        )

    def forward(j):
        hear(sends[NEARS + j])
        go(forwards[j])

    def first_matmul(c):
        pre = jnp.dot(x_in[pl.ds(c * CHUNK, CHUNK), :], w_in[...], preferred_element_type=F32)
        hidden[...] = jax.nn.gelu(pre, approximate=True).astype(BF16)

    def second_matmul(c):
        out[pl.ds(c * CHUNK, CHUNK), :] = jnp.dot(
            hidden[...], w_out[...], preferred_element_type=F32
        ).astype(BF16)

    to_owner, back = [], []
    for j in range(OWNED):
        sign = 1 if j % 2 == 0 else -1
        to_owner.append(
            remote(
                out.at[block(GUEST_SLOT[j]), :],
                partner.at[block(j), :],
                pr_send.at[j],
                pr_recv.at[j],
                (dp, at_y(-sign)),
            )
        )
        dx, dz = owned(j)
        back.append(
            remote(
                out.at[block(OWN_SLOT[j]), :],
                ret.at[block(1 + NEARS + j), :],
                rt_send.at[NEARS + j],
                rt_recv.at[NEARS + j],
                (at_xz(-dx, -dz), ex),
            )
        )
    near_back = [
        remote(
            out.at[block(NEAR_SLOT[i]), :],
            ret.at[block(1 + i), :],
            rt_send.at[i],
            rt_recv.at[i],
            (at_xz(-dx, -dz), ex),
        )
        for i, (dx, dz) in enumerate(NEAR)
    ]

    def add_and_send(j):
        hear(to_owner[j])

        def one(cols):
            mine = out[block(OWN_SLOT[j]), cols].astype(F32)
            out[block(OWN_SLOT[j]), cols] = (
                mine + partner[block(j), cols].astype(F32)
            ).astype(BF16)

        column_tiles(width, 768, one)
        go(back[j])

    for i in range(3):
        hear(sends[i])
    own_in.wait()
    hear(swap_in)
    first_matmul(0)
    forward(0)
    own_out.wait()
    hear(swap_out)
    second_matmul(0)
    for i in range(3):
        go(near_back[i])
    ret[block(0), :] = out[block(0), :]
    forward(1)
    hear(sends[3])
    hear(sends[4])
    hear(forwards[0])
    first_matmul(1)
    forward(2)
    second_matmul(1)
    go(to_owner[0])
    go(near_back[3])
    go(near_back[4])
    hear(forwards[1])
    hear(forwards[2])
    first_matmul(2)
    forward(3)
    forward(4)
    add_and_send(0)
    second_matmul(2)
    go(to_owner[1])
    go(to_owner[2])
    hear(forwards[3])
    hear(forwards[4])
    first_matmul(3)
    second_matmul(3)
    go(to_owner[3])
    go(to_owner[4])
    for j in range(1, OWNED):
        add_and_send(j)

    for c in range(2 * SIDE):

        @pl.when(ex == c)
        def _():
            def one(r, carry):
                rows = pl.ds(pl.multiple_of(r * 64, 64), 64)
                base[rows, :] = tokens[rows, c * share : (c + 1) * share]
                return carry

            lax.fori_loop(0, tok_rows // 64, one, 0)

    near = [dp] + [at_xz(0, q) for q in range(1, SIDE)] + [at_xz(q, 0) for q in range(1, SIDE)]

    def note(i, carry):
        owner, new = owners[i], []
        for w, candidate in enumerate(near):
            count, held = carry[w][0], carry[w][1:]
            hit = owner == candidate
            held = [jnp.where(hit & (count == k), i, held[k]) for k in range(OWN_IMG)]
            new.append((count + hit.astype(jnp.int32), *held))
        return tuple(new)

    none = jnp.int32(-1)
    noted = lax.fori_loop(
        0, owners.shape[0], note, ((jnp.int32(0),) + (none,) * OWN_IMG,) * len(near)
    )
    for w in range(len(near)):
        for k in range(OWN_IMG):
            img[w * OWN_IMG + k] = noted[w][1 + k]

    for copy in near_back + back[:3]:
        hear(copy)
    partial[:, pl.ds(width, 128)] = jnp.zeros((tok_rows, 128), F32)

    def combine(first):
        rows = pl.ds(0, EARLY) if first else pl.ds(EARLY, pick.shape[0] - EARLY)

        def one(cols):
            value = lax.dot_general(
                pick[rows, :],
                ret[rows, cols],
                (((0,), (0,)), ((), ())),
                preferred_element_type=F32,
            )
            partial[:, cols] = value if first else partial[:, cols] + value

        column_tiles(width, 256, one)

    combine(True)
    for copy in back[3:]:
        hear(copy)
    combine(False)

    columns = 2 * SIDE
    imgs = tok_rows // PATCH
    part = PATCH // 2

    def row_blocks(p, body):
        for i in range(imgs):

            def one(r, carry):
                off = pl.multiple_of(r * 64, 64)
                body(
                    i,
                    off,
                    pl.ds(pl.multiple_of(i * PATCH + p * part + r * 64, 64), 64),
                    pl.ds(pl.multiple_of(i * part + r * 64, 64), 64),
                )
                return carry

            lax.fori_loop(0, part // 64, one, 0)

    to_pair = []
    for p in range(2):

        def cut(i, off, rows, to):
            for c in range(columns):
                split[c % 2, c // 2, p, to, :] = partial[
                    rows, c * share : c * share + 256
                ].astype(BF16)

        row_blocks(p, cut)
        to_pair.append(
            remote(
                split.at[1 - core, :, p],
                pair.at[:, p],
                rs_send.at[p],
                rs_recv.at[p],
                other_core,
            )
        )
        go(to_pair[-1])
    over_y = []
    for p in range(2):
        hear(to_pair[p])

        def add_pair(i, off, rows, to):
            for c in range(SIDE):
                summed[c, p, to, :] = (
                    split[core, c, p, to, :].astype(F32) + pair[c, p, to, :].astype(F32)
                ).astype(BF16)

        row_blocks(p, add_pair)
        for r in (1, 3, 2):
            over_y.append(
                remote(
                    summed.at[(y + r) % SIDE, p],
                    others.at[r - 1, p],
                    rs_send.at[2 + p * 3 + r - 1],
                    rs_recv.at[2 + p * 3 + r - 1],
                    (dp, at_y(r)),
                )
            )
            go(over_y[-1])
    tail = share - 128

    def along(h, first, step):
        if (h == 0) == first:
            return (at_xz(step, 0), ex)
        return (at_xz(0, step), ex)

    gathers = []
    for p in range(2):
        for copy in over_y[3 * p : 3 * p + 3]:
            hear(copy)

        def total_up(i, off, rows, to):
            total = summed[y, p, to, :].astype(F32)
            for k in range(SIDE - 1):
                total = total + others[k, p, to, :].astype(F32)
            at = pl.ds(off, 64)
            stage_a[p][0, i, at, :] = (total[:, :128] + base[rows, 0:128]).astype(BF16)
            stage_a[p][1, i, at, 0:tail] = (
                total[:, 128:share] + base[rows, 128:share]
            ).astype(BF16)

        row_blocks(p, total_up)
        for r in (1, 3, 2):
            for h in range(2):
                k = (p * 2 + h) * 3 + r - 1
                gathers.append(
                    remote(
                        stage_a[p].at[h, pl.ds(0, imgs)],
                        stage_a[p].at[h, pl.ds(imgs * r, imgs)],
                        da_send.at[k],
                        da_recv.at[k],
                        along(h, True, r),
                    )
                )
                go(gathers[-1])

    def source_of(w, j):
        index = img[w * OWN_IMG + j]
        held = jnp.maximum(index, 0)
        device = held // imgs
        return index, device // SIDE, device % SIDE, held % imgs

    delivers = []
    for p in range(2):
        for copy in gathers[6 * p : 6 * p + 6]:
            hear(copy)
        for q in (1, 3, 2, 0):
            for h in range(2):
                w = q if h == 0 or q == 0 else SIDE - 1 + q
                for j in range(OWN_IMG):
                    _, from_x, from_z, which = source_of(w, j)
                    r = (x - from_x + SIDE) % SIDE if h == 0 else (z - from_z + SIDE) % SIDE
                    value = stage_a[p][h, r * imgs + which]
                    if q == 0:
                        stage_b[p][h, j] = value
                    else:
                        message[h, p, q - 1, j] = value
                if q:
                    k = (p * 2 + h) * 3 + q - 1
                    delivers.append(
                        remote(
                            message.at[h, p, q - 1],
                            stage_b[p].at[h, pl.ds(OWN_IMG * q, OWN_IMG)],
                            db_send.at[k],
                            db_recv.at[k],
                            along(h, False, q),
                        )
                    )
                    go(delivers[-1])
    for p in range(2):
        for copy in delivers[6 * p : 6 * p + 6]:
            hear(copy)
        for j in range(OWN_IMG):
            index, from_x, from_z, _ = source_of(0, j)
            there = index >= 0
            rows = pl.ds(j * PATCH + p * part, part)
            first = stage_b[p][0, (z - from_z + SIDE) % SIDE * OWN_IMG + j].astype(F32)
            delivered[rows, 0:128] = jnp.where(there, first, 0.0).astype(BF16)
            second = stage_b[p][1, (x - from_x + SIDE) % SIDE * OWN_IMG + j].astype(F32)
            delivered[rows, 128:share] = jnp.where(there, second, 0.0)[:, :tail].astype(BF16)
    finish()


def shards(tokens, ln_gain, ln_bias, weight_in, weight_out, expert_ids, combine_weights, owner_ids):
    groups = lax.axis_size("dp")
    columns = lax.axis_size("expert")
    tok_rows, width = tokens.shape
    share = width // columns
    hidden = 2 * weight_in.shape[2]
    experts = weight_in.shape[0] * groups

    def vmem(shape, dtype=BF16):
        return pltpu.VMEM(shape, dtype)

    def sems(count):
        return pltpu.SemaphoreType.DMA((count,))

    whole = pl.BlockSpec(memory_space=pltpu.VMEM)
    scratch = [
        pltpu.SMEM((7 * OWN_IMG,), jnp.int32),
        vmem((tok_rows, share), F32),
        vmem((tok_rows, width)),
        vmem((experts, tok_rows), F32),
        vmem((11 * CAP, tok_rows)),
        vmem((SENT * CAP, width)),
        vmem((16 * CAP, width)),
        vmem((width, hidden)),
        vmem((hidden, width)),
        vmem((CHUNK, hidden)),
        vmem((16 * CAP, width)),
        vmem((OWNED * CAP, width)),
        vmem((11 * CAP, width)),
        vmem((tok_rows, width + 128), F32),
        vmem((2, SIDE, 2, tok_rows // 2, 256)),
        vmem((SIDE, 2, tok_rows // 2, 256)),
        vmem((SIDE, 2, tok_rows // 2, 256)),
        vmem((SIDE - 1, 2, tok_rows // 2, 256)),
        vmem((2, 8, PATCH // 2, 128)),
        vmem((2, 8, PATCH // 2, 128)),
        vmem((2, 2, SIDE - 1, OWN_IMG, PATCH // 2, 128)),
        vmem((2, SIDE * OWN_IMG, PATCH // 2, 128)),
        vmem((2, SIDE * OWN_IMG, PATCH // 2, 128)),
    ]
    for count in (2, 2, 2, 10, 10, 5, 5, 5, 5, 10, 10, 8, 8, 12, 12, 12, 12):
        scratch.append(sems(count))
    return pl.pallas_call(
        kernel,
        out_shape=jax.ShapeDtypeStruct((OWN_IMG * PATCH, share), BF16),
        in_specs=[pl.BlockSpec(memory_space=pltpu.SMEM)]
        + [whole] * 5
        + [pl.BlockSpec(memory_space=pl.ANY)] * 2,
        out_specs=whole,
        scratch_shapes=scratch,
        compiler_params=pltpu.CompilerParams(
            collective_id=0, has_side_effects=True, vmem_limit_bytes=67043328
        ),
    )(
        owner_ids.reshape(-1),
        tokens,
        ln_gain.reshape(-1, 128),
        ln_bias.reshape(-1, 128),
        expert_ids.T,
        combine_weights.T,
        weight_in,
        weight_out,
    ).astype(F32)


def solution(mesh):
    return jax.shard_map(
        shards,
        mesh=mesh,
        in_specs=(
            P("dp", None),
            P(),
            P(),
            P("dp", None, "expert"),
            P("dp", "expert", None),
            P("dp", None),
            P("dp", None),
            P(),
        ),
        out_specs=P("dp", "expert"),
        check_vma=False,
    )
```

```python
import jax
import jax.numpy as jnp
from jax import lax
from jax.experimental import pallas as pl
from jax.experimental.pallas import tpu as pltpu
from jax.sharding import PartitionSpec as P

MESH = pl.DeviceIdType.MESH
F32 = jnp.float32
BF16 = jnp.bfloat16

PATCH = 256
CAP = 80
OWN_IMG = 4
SIDE = 4
epsilon = 1e-06

NEAR = ((0, 1), (0, 3), (1, 0), (3, 0), (1, 3))
EVEN = ((2, 2), (3, 1), (3, 3), (1, 2), (2, 1))
ODD = ((1, 1), (0, 2), (2, 0), (2, 3), (3, 2))
NEARS, OWNED = 5, 5
NEAR_SLOT = (1, 2, 3, 4, 5)
OWN_SLOT = (6, 8, 9, 12, 13)
GUEST_SLOT = (7, 10, 11, 14, 15)
SENT = NEARS + OWNED
CHUNK = 4 * CAP
EARLY = 9 * CAP


def column_tiles(width, step, body):
    count = width // step

    def one(n, carry):
        body(pl.ds(pl.multiple_of(n * step, 128), step))
        return carry

    lax.fori_loop(0, count, one, 0)
    if count * step < width:
        body(pl.ds(count * step, width - count * step))


def block(index):
    return pl.ds(index * CAP, CAP)


def kernel(
    owners,
    tokens,
    gain,
    bias,
    ids_t,
    weights_t,
    weight_in,
    weight_out,
    delivered,
    img,
    base,
    normed,
    rank,
    pick,
    gathered,
    x_in,
    w_in,
    w_out,
    hidden,
    out,
    partner,
    ret,
    partial,
    split,
    pair,
    summed,
    others,
    stage_a0,
    stage_a1,
    message,
    stage_b0,
    stage_b1,
    local_sem,
    wx_send,
    wx_recv,
    go_send,
    go_recv,
    fw_send,
    fw_recv,
    pr_send,
    pr_recv,
    rt_send,
    rt_recv,
    rs_send,
    rs_recv,
    da_send,
    da_recv,
    db_send,
    db_recv,
):
    stage_a, stage_b = (stage_a0, stage_a1), (stage_b0, stage_b1)
    dp = lax.axis_index("dp")
    ex = lax.axis_index("expert")
    x, z = dp // SIDE, dp % SIDE
    y, core = ex // 2, ex % 2
    parity = y % 2
    tok_rows, width = tokens.shape
    local_hidden = weight_in.shape[2]
    share = delivered.shape[1]

    def at_xz(dx, dz):
        return ((x + dx + SIDE) % SIDE) * SIDE + (z + dz + SIDE) % SIDE

    def at_y(dy):
        return ((y + dy + SIDE) % SIDE) * 2 + core

    def owned(j):
        (ax, az), (bx, bz) = EVEN[j], ODD[j]
        return ax + parity * (bx - ax), az + parity * (bz - az)

    def remote(src, dst, send, recv, device):
        return pltpu.make_async_remote_copy(
            src_ref=src,
            dst_ref=dst,
            send_sem=send,
            recv_sem=recv,
            device_id=device,
            device_id_type=MESH,
        )

    started, heard = [], []

    def go(copy):
        copy.start()
        started.append(copy)

    def hear(copy):
        copy.wait_recv()
        heard.append(copy)

    def finish():
        for copy in started:
            copy.wait_send()


    barrier = pltpu.get_barrier_semaphore()
    peers = [(at_xz(dx, dz), ex) for dx in range(SIDE) for dz in range(SIDE) if dx or dz]
    peers += [(dp, at_y(dy)) for dy in range(1, SIDE)]
    peers += [(dp, y * 2 + 1 - core)]
    for peer in peers:
        pl.semaphore_signal(barrier, inc=1, device_id=peer, device_id_type=MESH)

    own_in = pltpu.make_async_copy(
        weight_in.at[core], w_in.at[:, pl.ds(0, local_hidden)], local_sem.at[0]
    )
    own_out = pltpu.make_async_copy(
        weight_out.at[core], w_out.at[pl.ds(0, local_hidden), :], local_sem.at[1]
    )
    own_in.start()
    own_out.start()

    lanes = [pl.ds(c * 128, 128) for c in range(width // 128)]

    def norm_rows(r, carry):
        rows = pl.ds(pl.multiple_of(r * 64, 64), 64)
        total = tokens[rows, lanes[0]]
        for cols in lanes[1:]:
            total = total + tokens[rows, cols]
        mean = jnp.sum(total, axis=1, keepdims=True) / width
        total = jnp.zeros((64, 128), F32)
        for cols in lanes:
            center = tokens[rows, cols] - mean
            total = total + center * center
        scale = lax.rsqrt(jnp.sum(total, axis=1, keepdims=True) / width + epsilon)
        for c, cols in enumerate(lanes):
            value = (tokens[rows, cols] - mean) * scale * gain[c : c + 1, :] + bias[c : c + 1, :]
            normed[rows, cols] = value.astype(BF16)
        return carry

    lax.fori_loop(0, tok_rows // 64, norm_rows, 0, unroll=2)

    pl.semaphore_wait(barrier, len(peers))

    other_core = (dp, y * 2 + 1 - core)
    swap_in = remote(
        weight_in.at[1 - core],
        w_in.at[:, pl.ds(local_hidden, local_hidden)],
        wx_send.at[0],
        wx_recv.at[0],
        other_core,
    )
    swap_out = remote(
        weight_out.at[1 - core],
        w_out.at[pl.ds(local_hidden, local_hidden), :],
        wx_send.at[1],
        wx_recv.at[1],
        other_core,
    )
    go(swap_in)
    go(swap_out)

    experts = rank.shape[0]
    wanted = lax.broadcasted_iota(jnp.int32, (experts, tok_rows), 0)
    named = (ids_t[0:1, :] == wanted) | (ids_t[1:2, :] == wanted)
    earlier = (
        lax.broadcasted_iota(jnp.int32, (tok_rows, tok_rows), 0)
        < lax.broadcasted_iota(jnp.int32, (tok_rows, tok_rows), 1)
    ).astype(F32).astype(BF16)
    before = jnp.dot(named.astype(F32).astype(BF16), earlier, preferred_element_type=F32)
    rank[...] = jnp.where(named, before, 200.0)

    displacements = [(0, 0), *NEAR] + [owned(j) for j in range(OWNED)]
    place = lax.broadcasted_iota(jnp.int32, (CAP, tok_rows), 0).astype(F32)

    def expert_of(i):
        return 2 * at_xz(*displacements[i]) + core

    def hit_rows(i):
        return rank[pl.ds(expert_of(i), 1), :] == place

    for i in range(1 + SENT):
        pick[block(i), :] = hit_rows(i).astype(F32).astype(BF16)

    sends = []
    for i in range(SENT):
        slot = (NEAR_SLOT + OWN_SLOT)[i]
        sends.append(
            remote(
                gathered.at[block(i), :],
                x_in.at[block(slot), :],
                go_send.at[i],
                go_recv.at[i],
                (at_xz(*displacements[i + 1]), ex),
            )
        )

    def gather(start, stop):
        rows = pl.ds(start * CAP, (stop - start) * CAP)
        to = pl.ds((start - 1) * CAP, (stop - start) * CAP)

        def one(cols):
            gathered[to, cols] = jnp.dot(
                pick[rows, :], normed[:, cols], preferred_element_type=F32
            ).astype(BF16)

        column_tiles(width, 256, one)

    for start, end in ((6, 7), (1, 4), (7, 8), (4, 6), (8, 1 + SENT)):
        gather(start, end)
        for i in range(start, end):
            go(sends[i - 1])

    def own_block(cols):
        x_in[block(0), cols] = jnp.dot(
            pick[block(0), :], normed[:, cols], preferred_element_type=F32
        ).astype(BF16)

    column_tiles(width, 256, own_block)

    for i in range(1 + SENT):
        chosen = jnp.where(ids_t[0:1, :] == expert_of(i), weights_t[0:1, :], weights_t[1:2, :])
        pick[block(i), :] = jnp.where(hit_rows(i), chosen, 0.0).astype(BF16)

    forwards = []
    for j in range(OWNED):
        sign = 1 if j % 2 == 0 else -1
        forwards.append(
            remote(
                x_in.at[block(OWN_SLOT[j]), :],
                x_in.at[block(GUEST_SLOT[j]), :],
                fw_send.at[j],
                fw_recv.at[j],
                (dp, at_y(sign)),
            )
        )

    def forward(j):
        hear(sends[NEARS + j])
        go(forwards[j])

    def first_matmul(c):
        pre = jnp.dot(x_in[pl.ds(c * CHUNK, CHUNK), :], w_in[...], preferred_element_type=F32)
        hidden[...] = jax.nn.gelu(pre, approximate=True).astype(BF16)

    def second_matmul(c):
        out[pl.ds(c * CHUNK, CHUNK), :] = jnp.dot(
            hidden[...], w_out[...], preferred_element_type=F32
        ).astype(BF16)

    to_owner, back = [], []
    for j in range(OWNED):
        sign = 1 if j % 2 == 0 else -1
        to_owner.append(
            remote(
                out.at[block(GUEST_SLOT[j]), :],
                partner.at[block(j), :],
                pr_send.at[j],
                pr_recv.at[j],
                (dp, at_y(-sign)),
            )
        )
        dx, dz = owned(j)
        back.append(
            remote(
                out.at[block(OWN_SLOT[j]), :],
                ret.at[block(1 + NEARS + j), :],
                rt_send.at[NEARS + j],
                rt_recv.at[NEARS + j],
                (at_xz(-dx, -dz), ex),
            )
        )
    near_back = [
        remote(
            out.at[block(NEAR_SLOT[i]), :],
            ret.at[block(1 + i), :],
            rt_send.at[i],
            rt_recv.at[i],
            (at_xz(-dx, -dz), ex),
        )
        for i, (dx, dz) in enumerate(NEAR)
    ]

    def add_and_send(j):
        hear(to_owner[j])

        def one(cols):
            mine = out[block(OWN_SLOT[j]), cols].astype(F32)
            out[block(OWN_SLOT[j]), cols] = (
                mine + partner[block(j), cols].astype(F32)
            ).astype(BF16)

        column_tiles(width, 768, one)
        go(back[j])

    forward(0)
    for i in range(3):
        hear(sends[i])
    own_in.wait()
    hear(swap_in)
    first_matmul(0)
    forward(1)
    own_out.wait()
    hear(swap_out)
    second_matmul(0)
    for i in range(3):
        go(near_back[i])
    ret[block(0), :] = out[block(0), :]
    hear(sends[3])
    hear(sends[4])
    hear(forwards[0])
    first_matmul(1)
    forward(2)
    second_matmul(1)
    go(to_owner[0])
    go(near_back[3])
    go(near_back[4])
    forward(3)
    hear(forwards[1])
    hear(forwards[2])
    first_matmul(2)
    forward(4)
    add_and_send(0)
    second_matmul(2)
    go(to_owner[1])
    go(to_owner[2])
    hear(forwards[3])
    hear(forwards[4])
    first_matmul(3)
    add_and_send(1)
    add_and_send(2)
    second_matmul(3)
    go(to_owner[3])
    go(to_owner[4])
    add_and_send(3)
    add_and_send(4)

    for c in range(2 * SIDE):

        @pl.when(ex == c)
        def _():
            def one(r, carry):
                rows = pl.ds(pl.multiple_of(r * 64, 64), 64)
                base[rows, :] = tokens[rows, c * share : (c + 1) * share]
                return carry

            lax.fori_loop(0, tok_rows // 64, one, 0)

    near = [dp] + [at_xz(0, q) for q in range(1, SIDE)] + [at_xz(q, 0) for q in range(1, SIDE)]

    def note(i, carry):
        owner, new = owners[i], []
        for w, candidate in enumerate(near):
            count, held = carry[w][0], carry[w][1:]
            hit = owner == candidate
            held = [jnp.where(hit & (count == k), i, held[k]) for k in range(OWN_IMG)]
            new.append((count + hit.astype(jnp.int32), *held))
        return tuple(new)

    none = jnp.int32(-1)
    noted = lax.fori_loop(
        0, owners.shape[0], note, ((jnp.int32(0),) + (none,) * OWN_IMG,) * len(near)
    )
    for w in range(len(near)):
        for k in range(OWN_IMG):
            img[w * OWN_IMG + k] = noted[w][1 + k]

    for copy in near_back + back[:3]:
        hear(copy)
    partial[:, pl.ds(width, 128)] = jnp.zeros((tok_rows, 128), F32)

    def combine(first):
        rows = pl.ds(0, EARLY) if first else pl.ds(EARLY, pick.shape[0] - EARLY)

        def one(cols):
            value = lax.dot_general(
                pick[rows, :],
                ret[rows, cols],
                (((0,), (0,)), ((), ())),
                preferred_element_type=F32,
            )
            partial[:, cols] = value if first else partial[:, cols] + value

        column_tiles(width, 256, one)

    combine(True)
    for copy in back[3:]:
        hear(copy)
    combine(False)

    columns = 2 * SIDE
    imgs = tok_rows // PATCH
    part = PATCH // 2

    def row_blocks(p, body):
        for i in range(imgs):

            def one(r, carry):
                off = pl.multiple_of(r * 64, 64)
                body(
                    i,
                    off,
                    pl.ds(pl.multiple_of(i * PATCH + p * part + r * 64, 64), 64),
                    pl.ds(pl.multiple_of(i * part + r * 64, 64), 64),
                )
                return carry

            lax.fori_loop(0, part // 64, one, 0)

    to_pair = []
    for p in range(2):

        def cut(i, off, rows, to):
            for c in range(columns):
                split[c % 2, c // 2, p, to, :] = partial[
                    rows, c * share : c * share + 256
                ].astype(BF16)

        row_blocks(p, cut)
        to_pair.append(
            remote(
                split.at[1 - core, :, p],
                pair.at[:, p],
                rs_send.at[p],
                rs_recv.at[p],
                other_core,
            )
        )
        go(to_pair[-1])
    over_y = []
    for p in range(2):
        hear(to_pair[p])

        def add_pair(i, off, rows, to):
            for c in range(SIDE):
                summed[c, p, to, :] = (
                    split[core, c, p, to, :].astype(F32) + pair[c, p, to, :].astype(F32)
                ).astype(BF16)

        row_blocks(p, add_pair)
        for r in (2, 1, 3):
            over_y.append(
                remote(
                    summed.at[(y + r) % SIDE, p],
                    others.at[r - 1, p],
                    rs_send.at[2 + p * 3 + r - 1],
                    rs_recv.at[2 + p * 3 + r - 1],
                    (dp, at_y(r)),
                )
            )
            go(over_y[-1])
    tail = share - 128

    def along(h, first, step):
        if (h == 0) == first:
            return (at_xz(step, 0), ex)
        return (at_xz(0, step), ex)

    gathers = []
    for p in range(2):
        for copy in over_y[3 * p : 3 * p + 3]:
            hear(copy)

        def total_up(i, off, rows, to):
            total = summed[y, p, to, :].astype(F32)
            for k in range(SIDE - 1):
                total = total + others[k, p, to, :].astype(F32)
            at = pl.ds(off, 64)
            stage_a[p][0, i, at, :] = (total[:, :128] + base[rows, 0:128]).astype(BF16)
            stage_a[p][1, i, at, 0:tail] = (
                total[:, 128:share] + base[rows, 128:share]
            ).astype(BF16)

        row_blocks(p, total_up)
        for r in (2, 1, 3):
            for h in range(2):
                k = (p * 2 + h) * 3 + r - 1
                gathers.append(
                    remote(
                        stage_a[p].at[h, pl.ds(0, imgs)],
                        stage_a[p].at[h, pl.ds(imgs * r, imgs)],
                        da_send.at[k],
                        da_recv.at[k],
                        along(h, True, r),
                    )
                )
                go(gathers[-1])

    def source_of(w, j):
        index = img[w * OWN_IMG + j]
        held = jnp.maximum(index, 0)
        device = held // imgs
        return index, device // SIDE, device % SIDE, held % imgs

    delivers = []
    for p in range(2):
        for copy in gathers[6 * p : 6 * p + 6]:
            hear(copy)
        for q in (2, 1, 3, 0):
            for h in range(2):
                w = q if h == 0 or q == 0 else SIDE - 1 + q
                for j in range(OWN_IMG):
                    _, from_x, from_z, which = source_of(w, j)
                    r = (x - from_x + SIDE) % SIDE if h == 0 else (z - from_z + SIDE) % SIDE
                    value = stage_a[p][h, r * imgs + which]
                    if q == 0:
                        stage_b[p][h, j] = value
                    else:
                        message[h, p, q - 1, j] = value
                if q:
                    k = (p * 2 + h) * 3 + q - 1
                    delivers.append(
                        remote(
                            message.at[h, p, q - 1],
                            stage_b[p].at[h, pl.ds(OWN_IMG * q, OWN_IMG)],
                            db_send.at[k],
                            db_recv.at[k],
                            along(h, False, q),
                        )
                    )
                    go(delivers[-1])
    for p in range(2):
        for copy in delivers[6 * p : 6 * p + 6]:
            hear(copy)
        for j in range(OWN_IMG):
            index, from_x, from_z, _ = source_of(0, j)
            there = index >= 0
            rows = pl.ds(j * PATCH + p * part, part)
            first = stage_b[p][0, (z - from_z + SIDE) % SIDE * OWN_IMG + j].astype(F32)
            delivered[rows, 0:128] = jnp.where(there, first, 0.0).astype(BF16)
            second = stage_b[p][1, (x - from_x + SIDE) % SIDE * OWN_IMG + j].astype(F32)
            delivered[rows, 128:share] = jnp.where(there, second, 0.0)[:, :tail].astype(BF16)
    finish()


def shards(tokens, ln_gain, ln_bias, weight_in, weight_out, expert_ids, combine_weights, owner_ids):
    groups = lax.axis_size("dp")
    columns = lax.axis_size("expert")
    tok_rows, width = tokens.shape
    share = width // columns
    hidden = 2 * weight_in.shape[2]
    experts = weight_in.shape[0] * groups

    def vmem(shape, dtype=BF16):
        return pltpu.VMEM(shape, dtype)

    def sems(count):
        return pltpu.SemaphoreType.DMA((count,))

    whole = pl.BlockSpec(memory_space=pltpu.VMEM)
    scratch = [
        pltpu.SMEM((7 * OWN_IMG,), jnp.int32),
        vmem((tok_rows, share), F32),
        vmem((tok_rows, width)),
        vmem((experts, tok_rows), F32),
        vmem((11 * CAP, tok_rows)),
        vmem((SENT * CAP, width)),
        vmem((16 * CAP, width)),
        vmem((width, hidden)),
        vmem((hidden, width)),
        vmem((CHUNK, hidden)),
        vmem((16 * CAP, width)),
        vmem((OWNED * CAP, width)),
        vmem((11 * CAP, width)),
        vmem((tok_rows, width + 128), F32),
        vmem((2, SIDE, 2, tok_rows // 2, 256)),
        vmem((SIDE, 2, tok_rows // 2, 256)),
        vmem((SIDE, 2, tok_rows // 2, 256)),
        vmem((SIDE - 1, 2, tok_rows // 2, 256)),
        vmem((2, 8, PATCH // 2, 128)),
        vmem((2, 8, PATCH // 2, 128)),
        vmem((2, 2, SIDE - 1, OWN_IMG, PATCH // 2, 128)),
        vmem((2, SIDE * OWN_IMG, PATCH // 2, 128)),
        vmem((2, SIDE * OWN_IMG, PATCH // 2, 128)),
    ]
    for count in (2, 2, 2, 10, 10, 5, 5, 5, 5, 10, 10, 8, 8, 12, 12, 12, 12):
        scratch.append(sems(count))
    return pl.pallas_call(
        kernel,
        out_shape=jax.ShapeDtypeStruct((OWN_IMG * PATCH, share), BF16),
        in_specs=[pl.BlockSpec(memory_space=pltpu.SMEM)]
        + [whole] * 5
        + [pl.BlockSpec(memory_space=pl.ANY)] * 2,
        out_specs=whole,
        scratch_shapes=scratch,
        compiler_params=pltpu.CompilerParams(
            collective_id=0, has_side_effects=True, vmem_limit_bytes=67043328
        ),
    )(
        owner_ids.reshape(-1),
        tokens,
        ln_gain.reshape(-1, 128),
        ln_bias.reshape(-1, 128),
        expert_ids.T,
        combine_weights.T,
        weight_in,
        weight_out,
    ).astype(F32)


def solution(mesh):
    return jax.shard_map(
        shards,
        mesh=mesh,
        in_specs=(
            P("dp", None),
            P(),
            P(),
            P("dp", None, "expert"),
            P("dp", "expert", None),
            P("dp", None),
            P("dp", None),
            P(),
        ),
        out_specs=P("dp", "expert"),
        check_vma=False,
    )
```
